32 devices in a mesh: tm: 8 (over z, core), net: 4 (over y, x).
Axes of the slice: x: 2, y: 2, z: 4, core: 2. Of those that a mesh axis runs over, the one named last changes fastest.
Arguments:
- ptdf: bfloat16 [16384, 4096], P('net'), may hold values from -0.09375 to 0.09375
- demand: float32 [4096, 512], P('net', 'tm'), may hold values from 0 to 2
- generation: float32 [4096, 512], P('net', 'tm'), may hold values from 0 to 2
- cost: float32 [4096, 512], P('net', 'tm'), may hold values from 0.2 to 4
- gen_cap: float32 [4096], P('net'), may hold values from 0.5 to 4
- storage: float32 [2048, 512], P('net', 'tm'), may hold values from -3 to 3
- wear: float32 [2048], P('net'), may hold values from 0.1 to 2
- initial_charge: float32 [2048], P('net'), may hold values from 0 to 2
- leakage: float32 [2048], P('net'), may hold values from 0.0005859375 to 0.05
- line_dual: float32 [16384, 512], P('net', 'tm'), may hold values from -3 to 3
- line_index: int32 [16384], P('net'), may hold values from 0 to 4095
- rating: float32 [4096], replicated, may hold values from 0.3 to 3
- storage_bus: int32 [2048], replicated, may hold values from 0 to 4095
- balance_dual: float32 [512], P('tm'), may hold values from -4 to 4
- hour_block: int32 [512], P('tm'), may hold values from 0 to 23
- block_price: float32 [24], replicated, may hold values from -4 to 4
Outputs:
- generation_next: float32 [4096, 512], P('net', 'tm')
- storage_next: float32 [2048, 512], P('net', 'tm')
- charge: float32 [2048, 512], P('net', 'tm')
- line_dual_next: float32 [16384, 512], P('net', 'tm')
- balance_price: float32 [512], P('tm')
The draws below stay inside these ranges and needn't reach their ends.
All inputs are finite; a program needn't handle non-finite values.
Results may differ from the reference program's by a relative error of at most 0.0028.
Values may be sent and summed in bfloat16 or wider, within the bound.
A program may use at most 128 MiB of HBM per device.

```python
import math
import jax
import jax.numpy as jnp
from jax import lax

NB = 4096
L = 16384
S = 2048
LINES = 4096
BLOCKS = 24
PASSES = 2
H = 512


def plant(array, key, least, largest):
    place = [jax.random.randint(jax.random.fold_in(key, axis), (), 0, length) for axis, length in enumerate(array.shape)]
    longest = array.shape.index(max(array.shape))
    neighbour = place[:longest] + [(place[longest] + 1) % array.shape[longest]] + place[longest + 1:]
    return array.at[tuple(place)].set(least).at[tuple(neighbour)].set(largest)


def block_levels(stream_key, dims, cuts, least, top_value):
    def one(dim, blocks):
        heights = jax.random.uniform(jax.random.fold_in(jax.random.fold_in(stream_key, 6), dim), (blocks,), jnp.float32, least / len(cuts), top_value / len(cuts))
        return jnp.repeat(jnp.exp(heights), dims[dim] // blocks).reshape((-1,) + (1,) * (len(dims) - dim - 1))

    gain = one(*cuts[0])
    for cut in cuts[1:]:
        gain = gain * one(*cut)
    return gain


def centred(key, dims, scale, most, cuts=(), dtype=jnp.bfloat16):
    factor_of = block_levels(key, dims, cuts, -0.22, 0.18) if cuts else 1.0
    array = jax.random.normal(key, dims, jnp.float32) * scale * factor_of
    return jnp.minimum(jnp.maximum(array, -most), most).astype(dtype)


def setup_inputs(seed: int = 0) -> dict:
    key_list = jax.random.split(jax.random.key(seed), 17)
    ptdf = centred(key_list[0], (L, NB), NB ** -0.5, 0.09375, ((0, 4),))
    demand = jnp.clip(2.0 * jax.random.uniform(key_list[1], (NB, H), jnp.float32) ** block_levels(key_list[1], (NB, H), ((0, 4), (1, 8)), -0.2, 0.2), 0.0, 2.0)
    generation = jnp.clip(2.0 * jax.random.uniform(key_list[2], (NB, H), jnp.float32) ** block_levels(key_list[2], (NB, H), ((0, 4), (1, 8)), -0.2, 0.2), 0.0, 2.0)
    cost = jnp.clip(jnp.exp(math.log(4.0) - 2.9957323 * jax.random.uniform(key_list[3], (NB, H), jnp.float32) ** block_levels(key_list[3], (NB, H), ((0, 4), (1, 8)), -0.2, 0.2)), 0.2, 4.0)
    gen_cap = jnp.clip(jnp.exp(math.log(4.0) - 2.0794415 * jax.random.uniform(key_list[4], (NB,), jnp.float32) ** block_levels(key_list[4], (NB,), ((0, 4),), -0.2, 0.2)), 0.5, 4.0)
    storage = centred(key_list[5], (S, H), 0.5, 3.0, ((0, 4), (1, 8)), jnp.float32)
    wear = jnp.clip(jnp.exp(math.log(2.0) - 2.9957323 * jax.random.uniform(key_list[6], (S,), jnp.float32) ** block_levels(key_list[6], (S,), ((0, 4),), -0.2, 0.2)), 0.1, 2.0)
    initial_charge = jnp.clip(2.0 * jax.random.uniform(key_list[7], (S,), jnp.float32) ** block_levels(key_list[7], (S,), ((0, 4),), -0.2, 0.2), 0.0, 2.0)
    leakage = jnp.clip(jnp.exp(math.log(0.05) - 4.446565 * jax.random.uniform(key_list[8], (S,), jnp.float32) ** block_levels(key_list[8], (S,), ((0, 4),), -0.2, 0.2)), 0.0005859375, 0.05)
    line_dual = centred(key_list[9], (L, H), 0.3, 3.0, ((0, 4), (1, 8)), jnp.float32)
    line_index = plant(jax.random.randint(key_list[10], (L,), 0, LINES), jax.random.fold_in(key_list[10], 1), 0, LINES - 1).astype(jnp.int32)
    rating = jnp.clip(jnp.exp(jax.random.uniform(key_list[11], (LINES,), jnp.float32, math.log(0.3), math.log(3.0))), 0.3, 3.0)
    storage_bus = plant(jax.random.randint(key_list[12], (S,), 0, NB), jax.random.fold_in(key_list[12], 1), 0, NB - 1).astype(jnp.int32)
    balance_dual = centred(key_list[13], (H,), 1.0, 4.0, ((0, 8),), jnp.float32)
    hour_block = plant(jax.random.randint(key_list[14], (H,), 0, BLOCKS), jax.random.fold_in(key_list[14], 1), 0, BLOCKS - 1).astype(jnp.int32)
    block_price = centred(key_list[15], (BLOCKS,), 1.0, 4.0, (), jnp.float32)
    return {"ptdf": ptdf, "demand": demand, "generation": generation, "cost": cost, "gen_cap": gen_cap, "storage": storage, "wear": wear, "initial_charge": initial_charge, "leakage": leakage, "line_dual": line_dual, "line_index": line_index, "rating": rating, "storage_bus": storage_bus, "balance_dual": balance_dual, "hour_block": hour_block, "block_price": block_price}


STEP = 0.1
BAL = 0.5
STEP_UNIT = 0.2
ETA = 0.0625


def product(left, right):
    return jnp.dot(left.astype(jnp.float32), right.astype(jnp.float32), precision=lax.Precision.HIGHEST)


def reference(ptdf, demand, generation, cost, gen_cap, storage, wear, initial_charge, leakage, line_dual, line_index, rating, storage_bus, balance_dual, hour_block, block_price):
    limit = rating[line_index][:, None]
    unit_columns = ptdf[:, storage_bus]
    unit_flow = product(unit_columns, storage.astype(jnp.bfloat16))
    unit_total = jnp.sum(storage, axis=0)
    gen = generation
    dual = line_dual
    price = balance_dual
    for turn in range(PASSES):
        injection = (gen - demand).astype(jnp.bfloat16)
        flows = product(ptdf, injection) + unit_flow
        shifted = flows + dual
        dual = shifted - jnp.clip(shifted, -limit, limit)
        pull = product(ptdf.T, dual.astype(jnp.bfloat16))
        trial = jnp.clip(gen - STEP * (cost - price[None, :] + pull), 0.0, gen_cap[:, None])
        mismatch = jnp.sum(trial - demand, axis=0) + unit_total
        gen = trial - mismatch[None, :] / NB
        price = price - BAL * mismatch / NB
    hour_price = block_price[hour_block]
    storage_next = jnp.clip(storage + STEP_UNIT * (price[None, :] + hour_price[None, :] - wear[:, None] * storage), -1.0, 1.0)
    keep = 1.0 - leakage

    def advance(carry, column):
        carry = keep * carry - ETA * column
        return carry, carry

    _, charge = lax.scan(advance, initial_charge, storage_next.T)
    return gen, storage_next, charge.T, dual, price
```

```python
import functools

import jax
import jax.numpy as jnp
from jax import lax
from jax.experimental import pallas as pl
from jax.experimental.pallas import tpu as pltpu
from jax.sharding import PartitionSpec as P

PASSES = 2
STEP = 0.1
BAL = 0.5
STEP_UNIT = 0.2
ETA = 0.0625
MESH = pl.DeviceIdType.MESH
NN = (((1,), (0,)), ((), ()))


def peer(me, step, count):
    other, bit = 0, 1
    while bit < count:
        mine = lax.rem(me // bit, 2)
        other = other + bit * ((1 - mine) if step & bit else mine)
        bit *= 2
    return other


def as_row(col):
    n = col.shape[0]
    eye = lax.broadcasted_iota(jnp.int32, (n, n), 0) == lax.broadcasted_iota(jnp.int32, (n, n), 1)
    return jnp.sum(jnp.where(eye, col, 0), axis=0, keepdims=True)


def as_col(row):
    n = row.shape[1]
    eye = lax.broadcasted_iota(jnp.int32, (n, n), 0) == lax.broadcasted_iota(jnp.int32, (n, n), 1)
    return jnp.sum(jnp.where(eye, row, 0), axis=1, keepdims=True)


def kernel(
    nets,
    spans,
    buses,
    groups,
    chunks,
    ptdf_hbm,
    line_dual_hbm,
    cost_hbm,
    demand_hbm,
    generation_hbm,
    cap_hbm,
    storage_hbm,
    wear_hbm,
    initial_hbm,
    leakage_hbm,
    line_index_hbm,
    rating_hbm,
    storage_bus_hbm,
    price_hbm,
    hour_block_hbm,
    block_price_hbm,
    gen_out,
    storage_out,
    charge_out,
    dual_out,
    price_out,
    ptdf,
    ptdf_t,
    hits,
    line_dual,
    cost,
    demand,
    generation,
    cap,
    storage,
    wear,
    initial,
    leakage,
    line_index,
    rating,
    storage_bus,
    price_in,
    hour_block,
    block_price,
    units,
    unit_cols,
    inj,
    inj_other,
    left,
    acc,
    row_sum,
    pull_acc,
    flow_send,
    flow_recv,
    dual_half,
    part_send,
    part_recv,
    limit,
    growth,
    weight,
    sums,
    lasts,
    load_sem,
    ptdf_sem,
    unit_sem,
    inj_sem,
    part_sem,
    flow_sem,
    dual_sem,
    row_sem,
    sum_sem,
    last_sem,
):
    f32, bf16 = jnp.float32, jnp.bfloat16
    me = lax.axis_index("net")
    place = lax.axis_index("tm")
    core = lax.rem(place, 2)
    twin = place + 1 - 2 * core
    hours, nb = demand.shape
    hb = nb // 2
    cw = hb // chunks
    rows = ptdf.shape[1]
    su = storage.shape[1]
    both = 2 * hours
    own, other = pl.ds(0, hours), pl.ds(hours, hours)

    def device(j, across):
        return {"net": peer(me, j, nets), "tm": twin if across else place}

    barrier = pltpu.get_barrier_semaphore()
    for j in range(1, nets):
        for across in (0, 1):
            pl.semaphore_signal(
                barrier, inc=1, device_id=device(j, across), device_id_type=MESH
            )
    for step in range(1, spans):
        pl.semaphore_signal(
            barrier, inc=1, device_id={"tm": lax.rem(place + step, spans)}, device_id_type=MESH
        )

    def load(slot, source, target):
        copy = pltpu.make_async_copy(source, target, load_sem.at[slot])
        copy.start()
        return copy

    load_storage = load(0, storage_hbm, storage)
    load_generation = load(1, generation_hbm, generation)
    load_demand = load(2, demand_hbm, demand)
    load_bus = load(3, storage_bus_hbm, storage_bus)

    def band(j):
        return pl.ds(j * cw, cw)

    load_ptdf = {}
    for c in range(chunks):
        for j in range(nets):
            first = pl.multiple_of(peer(me, j, nets) * nb + core * hb + c * cw, cw)
            load_ptdf[c, j] = pltpu.make_async_copy(
                ptdf_hbm.at[:, pl.ds(first, cw)],
                ptdf.at[c, :, band(j)],
                ptdf_sem.at[c * nets + j],
            )
            load_ptdf[c, j].start()
    load_small = [
        load(4 + k, source, target)
        for k, (source, target) in enumerate(
            (
                (line_index_hbm, line_index),
                (rating_hbm, rating),
                (price_hbm, price_in),
                (hour_block_hbm, hour_block),
                (block_price_hbm, block_price),
                (cap_hbm, cap),
                (wear_hbm, wear),
                (initial_hbm, initial),
                (leakage_hbm, leakage),
            )
        )
    ]
    load_dual = load(13, line_dual_hbm, line_dual)
    load_cost = load(14, cost_hbm, cost)

    def part_cols(h, c):
        side = core if h == 0 else 1 - core
        return pl.ds(pl.multiple_of(side * hb + c * cw, cw), cw)

    load_storage.wait()
    units[own, pl.ds(0, su)] = storage[...].astype(bf16)
    load_generation.wait()
    load_demand.wait()

    def put_injection(turn, c, h, value):
        if h == 0:
            inj[turn, c, own, band(0)] = value.astype(bf16)
        else:
            inj_other[turn, c] = value.astype(bf16)

    for c in range(chunks):
        for h in range(2):
            cols = part_cols(h, c)
            put_injection(0, c, h, generation[:, cols] - demand[:, cols])
    pl.semaphore_wait(barrier, 2 * (nets - 1) + spans - 1)

    pending = []

    def send(src, dst, sems, slot, target):
        copy = pltpu.make_async_remote_copy(
            src_ref=src,
            dst_ref=dst,
            send_sem=sems.at[0, slot],
            recv_sem=sems.at[1, slot],
            device_id=target,
            device_id_type=MESH,
        )
        copy.start()
        pending.append(copy)
        return copy

    def send_injection(turn, c):
        copies = []
        for j in range(nets - 1, -1, -1):
            for h, side in enumerate((own, other)):
                if j or h:
                    source = inj_other.at[turn, c] if h else inj.at[turn, c, own, band(0)]
                    copies.append(
                        send(
                            source,
                            inj.at[turn, c, side, band(j)],
                            inj_sem.at[turn, c],
                            2 * j + h,
                            device(j, h),
                        )
                    )
        return copies

    def unit_band(k):
        return pl.ds(k * su, su)

    unit_copies = [
        send(
            units.at[own, unit_band(0)],
            units.at[own, unit_band(j)],
            unit_sem,
            2 * j,
            device(j, 0),
        )
        for j in range(1, nets)
    ]
    passed_on = [
        send(
            units.at[own, unit_band(0)], units.at[other, unit_band(0)], unit_sem, 1, device(0, 1)
        )
    ]
    inj_copies = [send_injection(0, c) for c in range(chunks)]

    load_bus.wait()
    per = su // 128
    lane = lax.broadcasted_iota(jnp.int32, (128, 128), 1)
    for k in range(nets):

        def mark(i, carry, k=k):
            row = storage_bus[pl.ds(peer(me, k, nets) * per + i, 1), :].astype(f32)
            bus = jnp.transpose(jnp.broadcast_to(row, (128, 128)))
            r = pl.ds(pl.multiple_of(k * su + i * 128, 128), 128)
            for c in range(chunks):
                for j in range(nets):
                    for t in range(cw // 128):
                        base = peer(me, j, nets) * nb + core * hb + c * cw + t * 128
                        here = (lane + base).astype(f32)
                        hits[c, r, pl.ds(j * cw + t * 128, 128)] = jnp.where(
                            bus == here, 1.0, 0.0
                        ).astype(bf16)
            return carry

        lax.fori_loop(0, per, mark, 0)

    for copy in load_small:
        copy.wait()
    index = line_index[...]
    spot, group = lax.rem(index, 128), index // 128
    found = jnp.zeros(index.shape, f32)
    for q in range(rating.shape[0]):
        row = jnp.broadcast_to(rating[q : q + 1, :], index.shape)
        found = jnp.where(
            group == q,
            jnp.take_along_axis(row, spot, axis=1, mode="promise_in_bounds"),
            found,
        )
    limit[...] = found
    for c in range(chunks):
        left[c, pl.ds(both, 16), :] = jnp.ones((16, nets * cw), bf16)

    tb = min(1024, rows)

    def turn_over(c, j):
        load_ptdf[c, j].wait()

        def one(i, carry):
            r = pl.ds(pl.multiple_of(i * tb, tb), tb)
            for t in range(cw // 128):
                lanes = pl.ds(j * cw + t * 128, 128)
                ptdf_t[c, lanes, r] = jnp.transpose(ptdf[c, r, lanes])
            return carry

        lax.fori_loop(0, rows // tb, one, 0)

    for c in range(chunks):
        for j in range(nets):
            turn_over(c, j)
        if c == 0:
            for j in range(1, nets):
                unit_copies[j - 1].wait_recv()
                passed_on.append(
                    send(
                        units.at[own, unit_band(j)],
                        units.at[other, unit_band(j)],
                        unit_sem,
                        2 * j + 1,
                        device(0, 1),
                    )
                )

    unit_part = jnp.sum(storage[...], axis=1, keepdims=True)
    price = as_col(price_in[...])
    block = as_col(hour_block[...])
    kinds = block_price.shape[1]
    hour_price = jnp.sum(
        jnp.where(
            block == lax.broadcasted_iota(jnp.int32, (hours, kinds), 1), block_price[...], 0.0
        ),
        axis=1,
        keepdims=True,
    )

    for copy in passed_on:
        copy.wait_recv()
    for c in range(chunks):
        unit_cols[c] = lax.dot_general(
            units[...], hits[c], NN, preferred_element_type=f32
        ).astype(bf16)

    span_rows = rows // groups
    rb = min(2048, rows)
    load_dual.wait()
    load_cost.wait()
    row_copy, sum_copies, drop = None, [], None

    def total_of(turn):
        whole = sums[turn, 0]
        for j in range(1, nets):
            sum_copies[j - 1].wait_recv()
            whole = whole + sums[turn, j]
        return as_col(whole[0:1, :hours])

    for turn in range(PASSES):
        old = line_dual if turn == 0 else dual_out
        high = both + 16 if turn == 0 else both
        flow_copies, dual_copies = [], []

        def flow(c, r):
            got = lax.dot_general(
                left[c, pl.ds(0, high), :], ptdf_t[c, :, r], NN, preferred_element_type=f32
            )
            if c > 0:
                got = got + acc[pl.ds(0, high), r]
            return got

        for c in range(chunks):
            for copy in inj_copies[c]:
                copy.wait_recv()
            left[c, pl.ds(0, both), :] = inj[turn, c] + unit_cols[c]
            if c + 1 < chunks:
                for i in range(rows // rb):
                    r = pl.ds(i * rb, rb)
                    acc[pl.ds(0, high), r] = flow(c, r)
        if turn > 0:
            mismatch = total_of(turn - 1)
            price = price - BAL * mismatch / buses
            drop = jnp.broadcast_to(mismatch / buses, (hours, 128))
            if turn == 1:
                row_copy.wait_recv()

        def settle(g):
            flow_copies[g].wait_recv()
            for k in range(span_rows // 128):
                i = g * (span_rows // 128) + k
                r = pl.ds(i * 128, 128)
                bound = limit[i : i + 1, :]
                x = acc[pl.ds(0, hours), r] + flow_recv[turn, :, r] + old[:, r]
                if turn > 0:
                    x = x - (row_sum[0, 0:1, r] + row_sum[1, 0:1, r]) * drop
                dual = x - jnp.clip(x, -bound, bound)
                dual_out[:, r] = dual
                dual_half[turn, own, r] = dual.astype(bf16)
            r = pl.ds(g * span_rows, span_rows)
            dual_copies.append(
                send(
                    dual_half.at[turn, own, r],
                    dual_half.at[turn, other, r],
                    dual_sem.at[turn],
                    g,
                    device(0, 1),
                )
            )

        part_copies = {}

        def pull(g):
            dual_copies[g].wait_recv()
            r = pl.ds(g * span_rows, span_rows)
            for c in range(chunks):
                got = lax.dot_general(
                    dual_half[turn, :, r], ptdf[c, r, :], NN, preferred_element_type=f32
                )
                if g > 0:
                    got = got + pull_acc[c]
                if g + 1 < groups:
                    pull_acc[c] = got
                    continue
                pull_acc[c, own, band(0)] = got[:hours, :cw]
                part_send[turn, c] = got.astype(bf16)
                for j in range(nets - 1, -1, -1):
                    for h, side in enumerate((own, other)):
                        if j or h:
                            part_copies[c, j, h] = send(
                                part_send.at[turn, c, side, band(j)],
                                part_recv.at[turn, c, side, band(j)],
                                part_sem.at[turn, c],
                                2 * j + h,
                                device(j, h),
                            )

        for g in range(groups + 2):
            if g < groups:
                r = pl.ds(g * span_rows, span_rows)
                got = flow(chunks - 1, r)
                acc[pl.ds(0, hours), r] = got[:hours]
                flow_send[turn, :, r] = got[hours:both]
                if turn == 0:
                    row_sum[0, :, r] = got[both : both + 8]
                flow_copies.append(
                    send(
                        flow_send.at[turn, :, r],
                        flow_recv.at[turn, :, r],
                        flow_sem.at[turn],
                        g,
                        device(0, 1),
                    )
                )
            if g >= 2:
                settle(g - 2)
            if g == groups and groups > 1:
                pull(0)
        for g in range(1 if groups > 1 else 0, groups):
            pull(g)
        if turn == 0:
            row_copy = send(row_sum.at[0], row_sum.at[1], row_sem, 0, device(0, 1))
            keep = 1.0 - leakage[...]
            hour = lax.broadcasted_iota(jnp.int32, (hours, su), 0)
            up, down = jnp.ones((hours, su), f32), jnp.ones((hours, su), f32)
            factor, span = keep, 1
            while span <= hours:
                up = jnp.where(lax.rem((hour + 1) // span, 2) == 1, up * factor, up)
                down = jnp.where(
                    lax.rem((hours - 1 - hour) // span, 2) == 1, down * factor, down
                )
                factor = factor * factor
                span = span * 2
            growth[...] = up
            weight[...] = -ETA * down

        gen_old = generation if turn == 0 else gen_out
        gained = jnp.zeros((hours, cw), f32)
        inj_copies = []
        for c in range(chunks):
            for j in range(nets - 1, -1, -1):
                for h in range(2):
                    if j or h:
                        part_copies[c, j, h].wait_recv()
            for h, side in enumerate((own, other)):
                if h == 0:
                    total = pull_acc[c, own, band(0)]
                else:
                    total = part_recv[turn, c, side, band(0)].astype(f32)
                for j in range(1, nets):
                    total = total + part_recv[turn, c, side, band(j)].astype(f32)
                cols = part_cols(h, c)
                before = gen_old[:, cols]
                if turn > 0:
                    before = before - drop[:, :1]
                trial = jnp.clip(
                    before - STEP * (cost[:, cols] - price + total), 0.0, cap[:, cols]
                )
                gen_out[:, cols] = trial
                more = trial - demand[:, cols]
                gained = gained + more
                if turn + 1 < PASSES:
                    put_injection(turn + 1, c, h, more)
            if turn + 1 < PASSES:
                inj_copies.append(send_injection(turn + 1, c))
        part = unit_part + jnp.sum(gained, axis=1, keepdims=True)
        sums[turn, 0, :, pl.ds(0, hours)] = jnp.broadcast_to(as_row(part), (8, hours))
        sum_copies = [
            send(sums.at[turn, 0], sums.at[turn, j], sum_sem.at[turn], j, device(j, 0))
            for j in range(1, nets)
        ]

    mismatch = total_of(PASSES - 1)
    price = price - BAL * mismatch / buses
    stored = storage[...]
    stored = jnp.clip(
        stored + STEP_UNIT * (price + hour_price - wear[...] * stored), -1.0, 1.0
    )
    lasts[0] = jnp.broadcast_to(
        jnp.sum(weight[...] * stored, axis=0, keepdims=True), (8, su)
    )
    last_copies = [
        send(lasts.at[0], lasts.at[s], last_sem, s, {"tm": lax.rem(place + s, spans)})
        for s in range(1, spans)
    ]
    storage_out[...] = stored
    gen_out[...] = gen_out[...] - mismatch / buses
    price_out[...] = as_row(price)
    running = -ETA * stored
    hour = lax.broadcasted_iota(jnp.int32, (hours, su), 0)
    factor = 1.0 - leakage[...]
    span = 1
    while span < hours:
        moved = jnp.where(hour >= span, pltpu.roll(running, span, axis=0), 0.0)
        running = running + factor * moved
        factor = factor * factor
        span = span * 2
    block_keep = growth[hours - 1 :, :]
    for copy in last_copies:
        copy.wait_recv()
    entering = initial[...]
    for s in range(spans - 1, 0, -1):
        entering = jnp.where(s <= place, block_keep * entering + lasts[s, 0:1, :], entering)
    charge_out[...] = growth[...] * entering + running
    for copy in pending:
        copy.wait_send()


def write_out(*refs):
    count = (len(refs) - 1) // 2
    sems = refs[-1]
    copies = [
        pltpu.make_async_copy(refs[k], refs[count + k], sems.at[k]) for k in range(count)
    ]
    for copy in copies:
        copy.start()
    for copy in copies:
        copy.wait()


def per_device(
    ptdf,
    demand,
    generation,
    cost,
    gen_cap,
    storage,
    wear,
    initial_charge,
    leakage,
    line_dual,
    line_index,
    rating,
    storage_bus,
    balance_dual,
    hour_block,
    block_price,
):
    nets, spans = lax.axis_size("net"), lax.axis_size("tm")
    rows, _ = ptdf.shape
    nb, hours = demand.shape
    su = storage.shape[0]
    units = su * nets
    buses, hb = nb * nets, nb // 2
    groups = 4 if rows % 512 == 0 else 1
    chunks = 2 if hb % 512 == 0 else 1
    cw = hb // chunks
    wide = nets * cw
    both = 2 * hours
    f32, bf16 = jnp.float32, jnp.bfloat16
    vmem = pl.BlockSpec(memory_space=pltpu.VMEM)
    hbm = pl.BlockSpec(memory_space=pl.ANY)
    sem = pltpu.SemaphoreType.DMA
    shapes = ((hours, nb), (hours, su), (hours, su), (hours, rows), (1, hours))
    small = (
        line_index.reshape(-1, 128),
        rating.reshape(-1, 128),
        storage_bus.reshape(-1, 128),
        balance_dual[None, :],
        hour_block[None, :],
        block_price[None, :],
    )
    found = pl.pallas_call(
        functools.partial(kernel, nets, spans, buses, groups, chunks),
        out_shape=tuple(pltpu.VMEM(shape, f32) for shape in shapes),
        in_specs=[hbm] * 16,
        out_specs=(vmem,) * 5,
        scratch_shapes=[
            pltpu.VMEM((chunks, rows, wide), bf16),
            pltpu.VMEM((chunks, wide, rows), bf16),
            pltpu.VMEM((chunks, units, wide), bf16),
            pltpu.VMEM((hours, rows), f32),
            pltpu.VMEM((hours, nb), f32),
            pltpu.VMEM((hours, nb), f32),
            pltpu.VMEM((hours, nb), f32),
            pltpu.VMEM((1, nb), f32),
            pltpu.VMEM((hours, su), f32),
            pltpu.VMEM((1, su), f32),
            pltpu.VMEM((1, su), f32),
            pltpu.VMEM((1, su), f32),
        ]
        + [pltpu.VMEM(array.shape, array.dtype) for array in small]
        + [
            pltpu.VMEM((both, units), bf16),
            pltpu.VMEM((chunks, both, wide), bf16),
            pltpu.VMEM((PASSES, chunks, both, wide), bf16),
            pltpu.VMEM((PASSES, chunks, hours, cw), bf16),
            pltpu.VMEM((chunks, both + 16, wide), bf16),
            pltpu.VMEM((both + 16, rows), f32),
            pltpu.VMEM((2, 8, rows), f32),
            pltpu.VMEM((chunks, both, wide), f32),
            pltpu.VMEM((PASSES, hours, rows), f32),
            pltpu.VMEM((PASSES, hours, rows), f32),
            pltpu.VMEM((PASSES, both, rows), bf16),
            pltpu.VMEM((PASSES, chunks, both, wide), bf16),
            pltpu.VMEM((PASSES, chunks, both, wide), bf16),
            pltpu.VMEM((rows // 128, 128), f32),
            pltpu.VMEM((hours, su), f32),
            pltpu.VMEM((hours, su), f32),
            pltpu.VMEM((PASSES, nets, 8, 128), f32),
            pltpu.VMEM((spans, 8, su), f32),
            sem((15,)),
            sem((chunks * nets,)),
            sem((2, 2 * nets)),
            sem((PASSES, chunks, 2, 2 * nets)),
            sem((PASSES, chunks, 2, 2 * nets)),
            sem((PASSES, 2, groups)),
            sem((PASSES, 2, groups)),
            sem((2, 1)),
            sem((PASSES, 2, nets)),
            sem((2, spans)),
        ],
        compiler_params=pltpu.CompilerParams(
            collective_id=0, has_side_effects=True, vmem_limit_bytes=62 * 1000 * 1000
        ),
    )(
        ptdf,
        line_dual.T,
        cost.T,
        demand.T,
        generation.T,
        gen_cap[None, :],
        storage.T,
        wear[None, :],
        initial_charge[None, :],
        leakage[None, :],
        *small,
    )
    gen, stored, charge, dual, price = pl.pallas_call(
        write_out,
        out_shape=tuple(jax.ShapeDtypeStruct(shape, f32) for shape in shapes),
        in_specs=[vmem] * 5,
        out_specs=(hbm,) * 5,
        scratch_shapes=[sem((5,))],
        compiler_params=pltpu.CompilerParams(vmem_limit_bytes=16 * 1000 * 1000),
    )(*found)
    return (gen.T, stored.T, charge.T, dual.T, price[0])


def solution(mesh):
    in_specs = (
        P("net", None),
        P("net", "tm"),
        P("net", "tm"),
        P("net", "tm"),
        P("net"),
        P("net", "tm"),
        P("net"),
        P("net"),
        P("net"),
        P("net", "tm"),
        P("net"),
        P(),
        P(),
        P("tm"),
        P("tm"),
        P(),
    )
    out_specs = (P("net", "tm"), P("net", "tm"), P("net", "tm"), P("net", "tm"), P("tm"))
    return jax.shard_map(
        per_device, mesh=mesh, in_specs=in_specs, out_specs=out_specs, check_vma=False
    )
```

```python
import functools

import jax
import jax.numpy as jnp
from jax import lax
from jax.experimental import pallas as pl
from jax.experimental.pallas import tpu as pltpu
from jax.sharding import PartitionSpec as P

PASSES = 2
STEP = 0.1
BAL = 0.5
STEP_UNIT = 0.2
ETA = 0.0625
MESH = pl.DeviceIdType.MESH
NT = (((1,), (1,)), ((), ()))
NN = (((1,), (0,)), ((), ()))


def peer(me, step, count):
    other, bit = 0, 1
    while bit < count:
        mine = lax.rem(me // bit, 2)
        other = other + bit * ((1 - mine) if step & bit else mine)
        bit *= 2
    return other


def as_row(col):
    n = col.shape[0]
    eye = lax.broadcasted_iota(jnp.int32, (n, n), 0) == lax.broadcasted_iota(jnp.int32, (n, n), 1)
    return jnp.sum(jnp.where(eye, col, 0), axis=0, keepdims=True)


def as_col(row):
    n = row.shape[1]
    eye = lax.broadcasted_iota(jnp.int32, (n, n), 0) == lax.broadcasted_iota(jnp.int32, (n, n), 1)
    return jnp.sum(jnp.where(eye, row, 0), axis=1, keepdims=True)


def kernel(
    nets,
    spans,
    buses,
    groups,
    chunks,
    ptdf_hbm,
    line_dual_hbm,
    cost_hbm,
    demand_hbm,
    generation_hbm,
    cap_hbm,
    storage_hbm,
    wear_hbm,
    initial_hbm,
    leakage_hbm,
    line_index_hbm,
    rating_hbm,
    storage_bus_hbm,
    price_hbm,
    hour_block_hbm,
    block_price_hbm,
    gen_out,
    storage_out,
    charge_out,
    dual_out,
    price_out,
    ptdf,
    ptdf_t,
    hits,
    line_dual,
    cost,
    demand,
    generation,
    cap,
    storage,
    wear,
    initial,
    leakage,
    line_index,
    rating,
    storage_bus,
    price_in,
    hour_block,
    block_price,
    units,
    unit_cols,
    inj,
    inj_other,
    left,
    acc,
    row_sum,
    pull_acc,
    flow_send,
    flow_recv,
    dual_half,
    part_send,
    part_recv,
    limit,
    growth,
    weight,
    sums,
    lasts,
    load_sem,
    ptdf_sem,
    unit_sem,
    inj_sem,
    part_sem,
    flow_sem,
    dual_sem,
    row_sem,
    sum_sem,
    last_sem,
):
    f32, bf16 = jnp.float32, jnp.bfloat16
    me = lax.axis_index("net")
    place = lax.axis_index("tm")
    core = lax.rem(place, 2)
    twin = place + 1 - 2 * core
    hours, nb = demand.shape
    hb = nb // 2
    cw = hb // chunks
    rows = ptdf.shape[1]
    su = storage.shape[1]
    both = 2 * hours
    own, other = pl.ds(0, hours), pl.ds(hours, hours)

    def device(j, across):
        return {"net": peer(me, j, nets), "tm": twin if across else place}

    barrier = pltpu.get_barrier_semaphore()
    for j in range(1, nets):
        for across in (0, 1):
            pl.semaphore_signal(
                barrier, inc=1, device_id=device(j, across), device_id_type=MESH
            )
    for step in range(1, spans):
        pl.semaphore_signal(
            barrier, inc=1, device_id={"tm": lax.rem(place + step, spans)}, device_id_type=MESH
        )

    def load(slot, source, target):
        copy = pltpu.make_async_copy(source, target, load_sem.at[slot])
        copy.start()
        return copy

    load_storage = load(0, storage_hbm, storage)
    load_generation = load(1, generation_hbm, generation)
    load_demand = load(2, demand_hbm, demand)
    load_bus = load(3, storage_bus_hbm, storage_bus)

    def band(j):
        return pl.ds(j * cw, cw)

    load_ptdf = {}
    for c in range(chunks):
        for j in range(nets):
            first = pl.multiple_of(peer(me, j, nets) * nb + core * hb + c * cw, cw)
            load_ptdf[c, j] = pltpu.make_async_copy(
                ptdf_hbm.at[:, pl.ds(first, cw)],
                ptdf.at[c, :, band(j)],
                ptdf_sem.at[c * nets + j],
            )
            load_ptdf[c, j].start()
    load_small = [
        load(4 + k, source, target)
        for k, (source, target) in enumerate(
            (
                (line_index_hbm, line_index),
                (rating_hbm, rating),
                (price_hbm, price_in),
                (hour_block_hbm, hour_block),
                (block_price_hbm, block_price),
                (cap_hbm, cap),
                (wear_hbm, wear),
                (initial_hbm, initial),
                (leakage_hbm, leakage),
            )
        )
    ]
    load_dual = load(13, line_dual_hbm, line_dual)
    load_cost = load(14, cost_hbm, cost)

    def part_cols(h, c):
        side = core if h == 0 else 1 - core
        return pl.ds(pl.multiple_of(side * hb + c * cw, cw), cw)

    load_storage.wait()
    units[own, pl.ds(0, su)] = storage[...].astype(bf16)
    load_generation.wait()
    load_demand.wait()

    def put_injection(turn, c, h, value):
        if h == 0:
            inj[turn, c, own, band(0)] = value.astype(bf16)
        else:
            inj_other[turn, c] = value.astype(bf16)

    for c in range(chunks):
        for h in range(2):
            cols = part_cols(h, c)
            put_injection(0, c, h, generation[:, cols] - demand[:, cols])
    pl.semaphore_wait(barrier, 2 * (nets - 1) + spans - 1)

    pending = []

    def send(src, dst, sems, slot, target):
        copy = pltpu.make_async_remote_copy(
            src_ref=src,
            dst_ref=dst,
            send_sem=sems.at[0, slot],
            recv_sem=sems.at[1, slot],
            device_id=target,
            device_id_type=MESH,
        )
        copy.start()
        pending.append(copy)
        return copy

    def send_injection(turn, c):
        copies = []
        for j in range(nets - 1, -1, -1):
            for h, side in enumerate((own, other)):
                if j or h:
                    source = inj_other.at[turn, c] if h else inj.at[turn, c, own, band(0)]
                    copies.append(
                        send(
                            source,
                            inj.at[turn, c, side, band(j)],
                            inj_sem.at[turn, c],
                            2 * j + h,
                            device(j, h),
                        )
                    )
        return copies

    def unit_band(k):
        return pl.ds(k * su, su)

    unit_copies = [
        send(
            units.at[own, unit_band(0)],
            units.at[own, unit_band(j)],
            unit_sem,
            2 * j,
            device(j, 0),
        )
        for j in range(1, nets)
    ]
    passed_on = [
        send(
            units.at[own, unit_band(0)], units.at[other, unit_band(0)], unit_sem, 1, device(0, 1)
        )
    ]
    inj_copies = [send_injection(0, c) for c in range(chunks)]

    load_bus.wait()
    per = su // 128
    lane = lax.broadcasted_iota(jnp.int32, (128, 128), 1)
    for k in range(nets):

        def mark(i, carry, k=k):
            row = storage_bus[pl.ds(peer(me, k, nets) * per + i, 1), :].astype(f32)
            bus = jnp.transpose(jnp.broadcast_to(row, (128, 128)))
            r = pl.ds(pl.multiple_of(k * su + i * 128, 128), 128)
            for c in range(chunks):
                for j in range(nets):
                    for t in range(cw // 128):
                        base = peer(me, j, nets) * nb + core * hb + c * cw + t * 128
                        here = (lane + base).astype(f32)
                        hits[c, r, pl.ds(j * cw + t * 128, 128)] = jnp.where(
                            bus == here, 1.0, 0.0
                        ).astype(bf16)
            return carry

        lax.fori_loop(0, per, mark, 0)

    for copy in load_small:
        copy.wait()
    index = line_index[...]
    spot, group = lax.rem(index, 128), index // 128
    found = jnp.zeros(index.shape, f32)
    for q in range(rating.shape[0]):
        row = jnp.broadcast_to(rating[q : q + 1, :], index.shape)
        found = jnp.where(
            group == q,
            jnp.take_along_axis(row, spot, axis=1, mode="promise_in_bounds"),
            found,
        )
    limit[...] = found
    for c in range(chunks):
        left[c, pl.ds(both, 16), :] = jnp.ones((16, nets * cw), bf16)

    tb = min(1024, rows)

    def turn_over(c, j):
        def one(i, carry):
            r = pl.ds(pl.multiple_of(i * tb, tb), tb)
            for t in range(cw // 128):
                lanes = pl.ds(j * cw + t * 128, 128)
                ptdf_t[c, lanes, r] = jnp.transpose(ptdf[c, r, lanes])
            return carry

        lax.fori_loop(0, rows // tb, one, 0)

    for j in range(1, nets):
        unit_copies[j - 1].wait_recv()
        passed_on.append(
            send(
                units.at[own, unit_band(j)],
                units.at[other, unit_band(j)],
                unit_sem,
                2 * j + 1,
                device(0, 1),
            )
        )

    unit_part = jnp.sum(storage[...], axis=1, keepdims=True)
    price = as_col(price_in[...])
    block = as_col(hour_block[...])
    kinds = block_price.shape[1]
    hour_price = jnp.sum(
        jnp.where(
            block == lax.broadcasted_iota(jnp.int32, (hours, kinds), 1), block_price[...], 0.0
        ),
        axis=1,
        keepdims=True,
    )

    for copy in passed_on:
        copy.wait_recv()
    for c in range(chunks):
        unit_cols[c] = lax.dot_general(
            units[...], hits[c], NN, preferred_element_type=f32
        ).astype(bf16)

    span_rows = rows // groups
    rb = rows
    load_dual.wait()
    load_cost.wait()
    row_copy, sum_copies, drop = None, [], None

    def total_of(turn):
        whole = sums[turn, 0]
        for j in range(1, nets):
            sum_copies[j - 1].wait_recv()
            whole = whole + sums[turn, j]
        return as_col(whole[0:1, :hours])

    for turn in range(PASSES):
        old = line_dual if turn == 0 else dual_out
        high = both + 16 if turn == 0 else both
        flow_copies, dual_copies = [], []

        def flow(c, r):
            rows_of, how = (ptdf[c, r, :], NT) if turn == 0 else (ptdf_t[c, :, r], NN)
            got = lax.dot_general(
                left[c, pl.ds(0, high), :], rows_of, how, preferred_element_type=f32
            )
            if c > 0:
                got = got + acc[pl.ds(0, high), r]
            return got

        for c in range(chunks):
            if turn == 0:
                for j in range(nets):
                    load_ptdf[c, j].wait()
            for copy in inj_copies[c]:
                copy.wait_recv()
            left[c, pl.ds(0, both), :] = inj[turn, c] + unit_cols[c]
            if c + 1 < chunks:
                for i in range(rows // rb):
                    r = pl.ds(i * rb, rb)
                    acc[pl.ds(0, high), r] = flow(c, r)
        if turn > 0:
            mismatch = total_of(turn - 1)
            price = price - BAL * mismatch / buses
            drop = jnp.broadcast_to(mismatch / buses, (hours, 128))
            if turn == 1:
                row_copy.wait_recv()

        def settle(g):
            flow_copies[g].wait_recv()
            for k in range(span_rows // 128):
                i = g * (span_rows // 128) + k
                r = pl.ds(i * 128, 128)
                bound = limit[i : i + 1, :]
                x = acc[pl.ds(0, hours), r] + flow_recv[turn, :, r] + old[:, r]
                if turn > 0:
                    x = x - (row_sum[0, 0:1, r] + row_sum[1, 0:1, r]) * drop
                dual = x - jnp.clip(x, -bound, bound)
                dual_out[:, r] = dual
                dual_half[turn, own, r] = dual.astype(bf16)
            r = pl.ds(g * span_rows, span_rows)
            dual_copies.append(
                send(
                    dual_half.at[turn, own, r],
                    dual_half.at[turn, other, r],
                    dual_sem.at[turn],
                    g,
                    device(0, 1),
                )
            )

        part_copies = {}

        def pull(g):
            dual_copies[g].wait_recv()
            r = pl.ds(g * span_rows, span_rows)
            for c in range(chunks):
                got = lax.dot_general(
                    dual_half[turn, :, r], ptdf[c, r, :], NN, preferred_element_type=f32
                )
                if g > 0:
                    got = got + pull_acc[c]
                if g + 1 < groups:
                    pull_acc[c] = got
                    continue
                pull_acc[c, own, band(0)] = got[:hours, :cw]
                part_send[turn, c] = got.astype(bf16)
                for j in range(nets - 1, -1, -1):
                    for h, side in enumerate((own, other)):
                        if j or h:
                            part_copies[c, j, h] = send(
                                part_send.at[turn, c, side, band(j)],
                                part_recv.at[turn, c, side, band(j)],
                                part_sem.at[turn, c],
                                2 * j + h,
                                device(j, h),
                            )

        for g in range(groups + 2):
            if g < groups:
                r = pl.ds(g * span_rows, span_rows)
                got = flow(chunks - 1, r)
                acc[pl.ds(0, hours), r] = got[:hours]
                flow_send[turn, :, r] = got[hours:both]
                if turn == 0:
                    row_sum[0, :, r] = got[both : both + 8]
                flow_copies.append(
                    send(
                        flow_send.at[turn, :, r],
                        flow_recv.at[turn, :, r],
                        flow_sem.at[turn],
                        g,
                        device(0, 1),
                    )
                )
            if g >= 2:
                settle(g - 2)
            if g == groups and groups > 1:
                pull(0)
        for g in range(1 if groups > 1 else 0, groups):
            pull(g)
        if turn == 0:
            row_copy = send(row_sum.at[0], row_sum.at[1], row_sem, 0, device(0, 1))
            keep = 1.0 - leakage[...]
            hour = lax.broadcasted_iota(jnp.int32, (hours, su), 0)
            up, down = jnp.ones((hours, su), f32), jnp.ones((hours, su), f32)
            factor, span = keep, 1
            while span <= hours:
                up = jnp.where(((hour + 1) & span) != 0, up * factor, up)
                down = jnp.where(((hours - 1 - hour) & span) != 0, down * factor, down)
                factor = factor * factor
                span = span * 2
            growth[...] = up
            weight[...] = -ETA * down

        gen_old = generation if turn == 0 else gen_out
        gained = jnp.zeros((hours, cw), f32)
        inj_copies = []
        for c in range(chunks):
            if turn == 0:
                for j in range(nets):
                    turn_over(c, j)
            for j in range(nets - 1, -1, -1):
                for h in range(2):
                    if j or h:
                        part_copies[c, j, h].wait_recv()
            for h, side in enumerate((own, other)):
                if h == 0:
                    total = pull_acc[c, own, band(0)]
                else:
                    total = part_recv[turn, c, side, band(0)].astype(f32)
                for j in range(1, nets):
                    total = total + part_recv[turn, c, side, band(j)].astype(f32)
                cols = part_cols(h, c)
                before = gen_old[:, cols]
                if turn > 0:
                    before = before - drop[:, :1]
                trial = jnp.clip(
                    before - STEP * (cost[:, cols] - price + total), 0.0, cap[:, cols]
                )
                gen_out[:, cols] = trial
                more = trial - demand[:, cols]
                gained = gained + more
                if turn + 1 < PASSES:
                    put_injection(turn + 1, c, h, more)
            if turn + 1 < PASSES:
                inj_copies.append(send_injection(turn + 1, c))
        part = unit_part + jnp.sum(gained, axis=1, keepdims=True)
        sums[turn, 0, :, pl.ds(0, hours)] = jnp.broadcast_to(as_row(part), (8, hours))
        sum_copies = [
            send(sums.at[turn, 0], sums.at[turn, j], sum_sem.at[turn], j, device(j, 0))
            for j in range(1, nets)
        ]

    mismatch = total_of(PASSES - 1)
    price = price - BAL * mismatch / buses
    stored = storage[...]
    stored = jnp.clip(
        stored + STEP_UNIT * (price + hour_price - wear[...] * stored), -1.0, 1.0
    )
    lasts[0] = jnp.broadcast_to(
        jnp.sum(weight[...] * stored, axis=0, keepdims=True), (8, su)
    )
    last_copies = [
        send(lasts.at[0], lasts.at[s], last_sem, s, {"tm": lax.rem(place + s, spans)})
        for s in range(1, spans)
    ]
    storage_out[...] = stored
    gen_out[...] = gen_out[...] - mismatch / buses
    price_out[...] = as_row(price)
    running = -ETA * stored
    hour = lax.broadcasted_iota(jnp.int32, (hours, su), 0)
    factor = 1.0 - leakage[...]
    span = 1
    while span < hours:
        moved = jnp.where(hour >= span, pltpu.roll(running, span, axis=0), 0.0)
        running = running + factor * moved
        factor = factor * factor
        span = span * 2
    block_keep = growth[hours - 1 :, :]
    for copy in last_copies:
        copy.wait_recv()
    entering = initial[...]
    for s in range(spans - 1, 0, -1):
        entering = jnp.where(s <= place, block_keep * entering + lasts[s, 0:1, :], entering)
    charge_out[...] = growth[...] * entering + running
    for copy in pending:
        copy.wait_send()


def write_out(*refs):
    count = (len(refs) - 1) // 2
    sems = refs[-1]
    copies = [
        pltpu.make_async_copy(refs[k], refs[count + k], sems.at[k]) for k in range(count)
    ]
    for copy in copies:
        copy.start()
    for copy in copies:
        copy.wait()


def per_device(
    ptdf,
    demand,
    generation,
    cost,
    gen_cap,
    storage,
    wear,
    initial_charge,
    leakage,
    line_dual,
    line_index,
    rating,
    storage_bus,
    balance_dual,
    hour_block,
    block_price,
):
    nets, spans = lax.axis_size("net"), lax.axis_size("tm")
    rows, _ = ptdf.shape
    nb, hours = demand.shape
    su = storage.shape[0]
    units = su * nets
    buses, hb = nb * nets, nb // 2
    groups = 4 if rows % 512 == 0 else 1
    chunks = 2 if hb % 512 == 0 else 1
    cw = hb // chunks
    wide = nets * cw
    both = 2 * hours
    f32, bf16 = jnp.float32, jnp.bfloat16
    vmem = pl.BlockSpec(memory_space=pltpu.VMEM)
    hbm = pl.BlockSpec(memory_space=pl.ANY)
    sem = pltpu.SemaphoreType.DMA
    shapes = ((hours, nb), (hours, su), (hours, su), (hours, rows), (1, hours))
    small = (
        line_index.reshape(-1, 128),
        rating.reshape(-1, 128),
        storage_bus.reshape(-1, 128),
        balance_dual[None, :],
        hour_block[None, :],
        block_price[None, :],
    )
    found = pl.pallas_call(
        functools.partial(kernel, nets, spans, buses, groups, chunks),
        out_shape=tuple(pltpu.VMEM(shape, f32) for shape in shapes),
        in_specs=[hbm] * 16,
        out_specs=(vmem,) * 5,
        scratch_shapes=[
            pltpu.VMEM((chunks, rows, wide), bf16),
            pltpu.VMEM((chunks, wide, rows), bf16),
            pltpu.VMEM((chunks, units, wide), bf16),
            pltpu.VMEM((hours, rows), f32),
            pltpu.VMEM((hours, nb), f32),
            pltpu.VMEM((hours, nb), f32),
            pltpu.VMEM((hours, nb), f32),
            pltpu.VMEM((1, nb), f32),
            pltpu.VMEM((hours, su), f32),
            pltpu.VMEM((1, su), f32),
            pltpu.VMEM((1, su), f32),
            pltpu.VMEM((1, su), f32),
        ]
        + [pltpu.VMEM(array.shape, array.dtype) for array in small]
        + [
            pltpu.VMEM((both, units), bf16),
            pltpu.VMEM((chunks, both, wide), bf16),
            pltpu.VMEM((PASSES, chunks, both, wide), bf16),
            pltpu.VMEM((PASSES, chunks, hours, cw), bf16),
            pltpu.VMEM((chunks, both + 16, wide), bf16),
            pltpu.VMEM((both + 16, rows), f32),
            pltpu.VMEM((2, 8, rows), f32),
            pltpu.VMEM((chunks, both, wide), f32),
            pltpu.VMEM((PASSES, hours, rows), f32),
            pltpu.VMEM((PASSES, hours, rows), f32),
            pltpu.VMEM((PASSES, both, rows), bf16),
            pltpu.VMEM((PASSES, chunks, both, wide), bf16),
            pltpu.VMEM((PASSES, chunks, both, wide), bf16),
            pltpu.VMEM((rows // 128, 128), f32),
            pltpu.VMEM((hours, su), f32),
            pltpu.VMEM((hours, su), f32),
            pltpu.VMEM((PASSES, nets, 8, 128), f32),
            pltpu.VMEM((spans, 8, su), f32),
            sem((15,)),
            sem((chunks * nets,)),
            sem((2, 2 * nets)),
            sem((PASSES, chunks, 2, 2 * nets)),
            sem((PASSES, chunks, 2, 2 * nets)),
            sem((PASSES, 2, groups)),
            sem((PASSES, 2, groups)),
            sem((2, 1)),
            sem((PASSES, 2, nets)),
            sem((2, spans)),
        ],
        compiler_params=pltpu.CompilerParams(
            collective_id=0, has_side_effects=True, vmem_limit_bytes=62 * 1000 * 1000
        ),
    )(
        ptdf,
        line_dual.T,
        cost.T,
        demand.T,
        generation.T,
        gen_cap[None, :],
        storage.T,
        wear[None, :],
        initial_charge[None, :],
        leakage[None, :],
        *small,
    )
    gen, stored, charge, dual, price = pl.pallas_call(
        write_out,
        out_shape=tuple(jax.ShapeDtypeStruct(shape, f32) for shape in shapes),
        in_specs=[vmem] * 5,
        out_specs=(hbm,) * 5,
        scratch_shapes=[sem((5,))],
        compiler_params=pltpu.CompilerParams(vmem_limit_bytes=16 * 1000 * 1000),
    )(*found)
    return (gen.T, stored.T, charge.T, dual.T, price[0])


def solution(mesh):
    in_specs = (
        P("net", None),
        P("net", "tm"),
        P("net", "tm"),
        P("net", "tm"),
        P("net"),
        P("net", "tm"),
        P("net"),
        P("net"),
        P("net"),
        P("net", "tm"),
        P("net"),
        P(),
        P(),
        P("tm"),
        P("tm"),
        P(),
    )
    out_specs = (P("net", "tm"), P("net", "tm"), P("net", "tm"), P("net", "tm"), P("tm"))
    return jax.shard_map(
        per_device, mesh=mesh, in_specs=in_specs, out_specs=out_specs, check_vma=False
    )
```
